256 devices in a mesh: seq: 32 (over z, x), blk: 8 (over y, core).
Axes of the slice: x: 4, y: 4, z: 8, core: 2. Of those that a mesh axis runs over, the one named last changes fastest.
Arguments:
- qkv: bfloat16 [32768, 12288], P(('seq', 'blk')), may hold values from -24 to 24
- kept_kv: bfloat16 [32, 2, 128, 4096], P('blk', None, None, 'seq'), may hold values from -24 to 24
- cur_list: int32 [256, 8], replicated, may hold values from 0 to 255, as said below
- kept_list: int32 [256, 12], replicated, may hold values from 0 to 31, as said below
- kept_count: int32 [256], replicated, may hold values from 1 to 12, as said below
Outputs:
- attn_out: bfloat16 [32768, 4096], P(('seq', 'blk'))
The draws below stay inside these ranges and needn't reach their ends.
Inputs may be any that keep to these rules, and one draw needn't show every extreme that they name: `cur_list`: row t lists 8 different tiles t2 of tile t's spatial region, that is with (t2) % 8 equal to (t) % 8; the first entry is t itself. `kept_list`: each row names 12 different kept blocks. `kept_count`: some tile uses all 12 slots.
All inputs are finite; a program needn't handle non-finite values.
Results may differ from the reference program's by a relative error of at most 0.0025.
Values may be sent and summed in bfloat16 or wider, within the bound.
A program may use at most 64 MiB of HBM per device.

```python
import math
import jax
import jax.numpy as jnp
from jax import lax

HEAD_DIM = 128
HEADS = 32
TILE = 128
TILES_DEV = 1
REGIONS = 8
REGION_TILES = 32
TILES = 256
TOKENS = 32768
CUR_BLOCKS = 8
KEPT = 32
WINDOW = 12


def draw_qkv(key, part):
    key_base, key_scale = jax.random.split(key, 2)
    shape = (TOKENS, 3, HEADS * HEAD_DIM)
    base = jax.random.normal(key_base, shape, jnp.float32)
    log_scale = jax.random.uniform(key_scale, (TOKENS, 3, 1), jnp.float32, math.log(0.3), math.log(3.0))
    is_query = (jnp.arange(3) == 0)[None, :, None]
    factor = jnp.where(is_query, 1.0, jnp.exp(log_scale))
    values = jnp.clip(base * factor, -24.0, 24.0)
    return values.reshape(TOKENS, 3 * HEADS * HEAD_DIM).astype(jnp.bfloat16)


def draw_kept_kv(key, part):
    key_base, key_scale = jax.random.split(key, 2)
    shape = (KEPT, 2, TILE, HEADS * HEAD_DIM)
    base = jax.random.normal(key_base, shape, jnp.float32)
    log_scale = jax.random.uniform(key_scale, (KEPT, 2, TILE, 1), jnp.float32, math.log(0.3), math.log(3.0))
    return jnp.clip(base * jnp.exp(log_scale), -24.0, 24.0).astype(jnp.bfloat16)


def draw_cur_list(key, part):
    tile_keys = jax.random.split(key, TILES)
    tile_ids = jnp.arange(TILES, dtype=jnp.int32)

    def one_tile(tile_key, tile_id):
        own_place = tile_id // TILES_DEV // REGIONS * TILES_DEV + tile_id % TILES_DEV
        region = tile_id // TILES_DEV % REGIONS
        others = (own_place + 1 + jax.random.permutation(tile_key, REGION_TILES - 1)[:CUR_BLOCKS - 1]) % REGION_TILES
        places = jnp.concatenate([own_place[None], others.astype(jnp.int32)])
        return (places // TILES_DEV * REGIONS + region) * TILES_DEV + places % TILES_DEV
    return jax.vmap(one_tile)(tile_keys, tile_ids).astype(jnp.int32)


def draw_kept_list(key, part):
    tile_keys = jax.random.split(key, TILES)
    return jax.vmap(lambda tile_key: jax.random.permutation(tile_key, KEPT)[:WINDOW])(tile_keys).astype(jnp.int32)


def draw_kept_count(key, part):
    key_first, key_second, key_full = jax.random.split(key, 3)
    first = jax.random.randint(key_first, (TILES,), 0, WINDOW)
    second = jax.random.randint(key_second, (TILES,), 0, WINDOW)
    counts = 1 + first * second // WINDOW
    full_tile = jax.random.randint(key_full, (), 0, TILES)
    return counts.at[full_tile].set(WINDOW).astype(jnp.int32)


def setup_inputs(seed: int = 0) -> dict:
    streams_of = jax.random.split(jax.random.key(seed), 6)
    return {
        "qkv": draw_qkv(jax.random.fold_in(streams_of[5], 71), 0),
        "kept_kv": draw_kept_kv(jax.random.fold_in(streams_of[5], 71), 0),
        "cur_list": draw_cur_list(jax.random.fold_in(streams_of[5], 71), 0),
        "kept_list": draw_kept_list(jax.random.fold_in(streams_of[5], 71), 0),
        "kept_count": draw_kept_count(jax.random.fold_in(streams_of[5], 71), 0),
    }


MASKED_SCORE = -1e+30

def reference(qkv, kept_kv, cur_list, kept_list, kept_count):
    tiles_all = qkv.reshape(TILES, TILE, 3, HEADS, HEAD_DIM)
    kept_all = kept_kv.reshape(KEPT, 2, TILE, HEADS, HEAD_DIM)
    score_scale = 1.0 / math.sqrt(HEAD_DIM)

    def one_tile(inputs):
        tile_index, cur_sel, kept_sel, slot_count = inputs
        own_tile = lax.dynamic_index_in_dim(tiles_all, tile_index, 0, keepdims=False)
        queries = own_tile[:, 0].astype(jnp.float32)
        near_blocks = tiles_all[cur_sel]
        far_blocks = kept_all[kept_sel]
        keys = jnp.concatenate([near_blocks[:, :, 1].reshape(-1, HEADS, HEAD_DIM), far_blocks[:, 0].reshape(-1, HEADS, HEAD_DIM)], 0).astype(jnp.float32)
        values = jnp.concatenate([near_blocks[:, :, 2].reshape(-1, HEADS, HEAD_DIM), far_blocks[:, 1].reshape(-1, HEADS, HEAD_DIM)], 0).astype(jnp.float32)
        is_live = jnp.concatenate([jnp.ones((CUR_BLOCKS * TILE,), dtype=bool), jnp.repeat(jnp.arange(WINDOW) < slot_count, TILE)])
        scores = jnp.einsum('ihd,khd->hik', queries, keys) * score_scale
        scores = jnp.where(is_live, scores, MASKED_SCORE)
        row_max = scores.max(axis=-1, keepdims=True)
        weights = jnp.where(is_live, jnp.exp(scores - row_max), 0.0)
        row_total = weights.sum(axis=-1)
        rounded = lax.optimization_barrier(weights.astype(jnp.bfloat16)).astype(jnp.float32)
        mixture = jnp.einsum('hik,khd->ihd', rounded, values)
        result = mixture / jnp.transpose(row_total)[:, :, None]
        return result.astype(jnp.bfloat16).reshape(TILE, HEADS * HEAD_DIM)
    tile_indices = jnp.arange(TILES, dtype=jnp.int32)
    output = lax.map(one_tile, (tile_indices, cur_list, kept_list, kept_count))
    return output.reshape(TOKENS, HEADS * HEAD_DIM)
```

```python
import functools
import math

import jax
import jax.numpy as jnp
from jax import lax
from jax.experimental import pallas as pl
from jax.experimental.pallas import tpu as pltpu
from jax.sharding import PartitionSpec as P

HEAD_DIM = 128
MASKED_SCORE = -1e30
MESH = pl.DeviceIdType.MESH
LOG2_E = 1.4426950408889634


def kernel(
    seq_count,
    blk_count,
    cur_ref,
    kept_list_ref,
    count_ref,
    qkv_ref,
    kept_ref,
    out_ref,
    stage,
    q_all,
    k_all,
    v_all,
    kept_all,
    scores,
    weights,
    partial,
    totals,
    mixed,
    stage_sem,
    kept_send,
    kept_recv,
    k_send,
    k_recv,
    q_send,
    q_recv,
    v_send,
    v_recv,
    o_send,
    o_recv,
):
    me = lax.axis_index("seq")
    region = lax.axis_index("blk")
    near_count = cur_ref.shape[0]
    window = kept_list_ref.shape[0]
    kept_own = kept_ref.shape[0]
    width = HEAD_DIM
    factor = LOG2_E / math.sqrt(width)

    order = (1, 0, 2)

    def stage_copy(slot, group, head):
        column = pl.multiple_of((group * seq_count + head) * width, width)
        return pltpu.make_async_copy(
            qkv_ref.at[:, pl.ds(column, width)], stage.at[slot, head], stage_sem.at[slot]
        )

    for slot, group in enumerate(order):

        @pl.loop(0, seq_count)
        def _(head, slot=slot, group=group):
            stage_copy(slot, group, head).start()

    barrier = pltpu.get_barrier_semaphore()

    @pl.loop(1, seq_count)
    def _(step):
        pl.semaphore_signal(
            barrier, inc=1, device_id={"seq": lax.rem(me + step, seq_count)}, device_id_type=MESH
        )

    @pl.loop(1, blk_count)
    def _(step):
        pl.semaphore_signal(
            barrier, inc=1, device_id={"blk": lax.rem(region + step, blk_count)}, device_id_type=MESH
        )

    pl.semaphore_wait(barrier, seq_count - 1 + blk_count - 1)

    buffers = (k_all, q_all, v_all)
    sends = (k_send, q_send, v_send)
    recvs = (k_recv, q_recv, v_recv)

    def send_group(slot):
        pltpu.make_async_copy(stage.at[slot], stage.at[slot], stage_sem.at[slot]).wait()
        target, send, recv = buffers[slot], sends[slot], recvs[slot]
        recv_mine = recv.at[me] if slot == 1 else recv
        pltpu.make_async_copy(stage.at[slot, me], target.at[me], recv_mine).start()

        @pl.loop(1, seq_count)
        def _(step):
            other = lax.rem(me + step, seq_count)
            pltpu.make_async_remote_copy(
                src_ref=stage.at[slot, other],
                dst_ref=target.at[me],
                send_sem=send,
                recv_sem=recv_mine,
                device_id={"seq": other},
                device_id_type=MESH,
            ).start()

    send_group(0)
    kept_mine = pl.ds(region * kept_own, kept_own)
    pltpu.make_async_copy(kept_ref, kept_all.at[kept_mine], kept_recv).start()

    @pl.loop(1, blk_count)
    def _(step):
        other = lax.rem(region + step, blk_count)
        pltpu.make_async_remote_copy(
            src_ref=kept_ref,
            dst_ref=kept_all.at[kept_mine],
            send_sem=kept_send,
            recv_sem=kept_recv,
            device_id={"blk": other},
            device_id_type=MESH,
        ).start()

    send_group(1)
    send_group(2)

    pltpu.make_async_copy(k_all, k_all, k_recv).wait()
    pltpu.make_async_copy(kept_all, kept_all, kept_recv).wait()

    contract_last = (((1,), (1,)), ((), ()))

    @pl.loop(0, seq_count)
    def _(step):
        tile = lax.rem(me + seq_count - step, seq_count)
        pltpu.make_async_copy(q_all.at[tile], q_all.at[tile], q_recv.at[tile]).wait()
        row = tile * blk_count + region
        queries = q_all[tile]
        live = count_ref[row]
        top = None
        for pair in range((near_count + window) // 2):
            first = 2 * pair
            if first < near_count:
                ids = [cur_ref[first + n, row] // blk_count for n in range(2)]
                keys = [k_all[i] for i in ids]
            else:
                slots = [first - near_count + n for n in range(2)]
                keys = [kept_all[kept_list_ref[w, row], 0] for w in slots]
            product = lax.dot_general(
                queries,
                jnp.concatenate(keys, axis=0),
                contract_last,
                preferred_element_type=jnp.float32,
            )
            for n in range(2):
                part = product[:, n * width : (n + 1) * width]
                if first >= near_count + 1 or (first >= near_count and n > 0):
                    part = part + jnp.where(first - near_count + n < live, 0.0, MASKED_SCORE)
                scores[:, pl.ds((first + n) * width, width)] = part
                top = part if top is None else jnp.maximum(top, part)
        row_max = jnp.max(top, axis=1, keepdims=True)
        total = None
        mixture = None
        for pair in range((near_count + window) // 2):
            first = 2 * pair
            weight = jnp.exp2((scores[:, pl.ds(first * width, 2 * width)] - row_max) * factor)
            half = weight[:, :width] + weight[:, width:]
            total = half if total is None else total + half
            rounded = weight.astype(jnp.bfloat16)
            if first < near_count:
                weights[tile, :, pl.ds(first * width, 2 * width)] = rounded
            else:
                slots = [first - near_count + n for n in range(2)]
                values = [kept_all[kept_list_ref[w, row], 1] for w in slots]
                term = jnp.dot(
                    rounded, jnp.concatenate(values, axis=0), preferred_element_type=jnp.float32
                )
                mixture = term if mixture is None else mixture + term
        totals[tile] = jnp.broadcast_to(jnp.sum(total, axis=1, keepdims=True), totals.shape[1:])
        partial[tile] = mixture

    pltpu.make_async_copy(v_all, v_all, v_recv).wait()

    columns_mine = pl.ds(pl.multiple_of(me * width, width), width)

    def send_out(tile):
        pltpu.make_async_remote_copy(
            src_ref=mixed.at[tile],
            dst_ref=out_ref.at[:, columns_mine],
            send_sem=o_send,
            recv_sem=o_recv,
            device_id={"seq": tile},
            device_id_type=MESH,
        ).start()

    @pl.loop(1, seq_count + 1)
    def _(step):
        tile = lax.rem(me + step, seq_count)
        row = tile * blk_count + region
        mixture = partial[tile]
        for pair in range(near_count // 2):
            first = 2 * pair
            values = [v_all[cur_ref[first + n, row] // blk_count] for n in range(2)]
            mixture = mixture + jnp.dot(
                weights[tile, :, pl.ds(first * width, 2 * width)],
                jnp.concatenate(values, axis=0),
                preferred_element_type=jnp.float32,
            )
        mixed[tile] = (mixture / totals[tile]).astype(jnp.bfloat16)

        @pl.when(step > 1)
        def _():
            send_out(lax.rem(me + step - 1, seq_count))

    own_copy = pltpu.make_async_copy(mixed.at[me], out_ref.at[:, columns_mine], o_recv)
    own_copy.start()

    others = pl.ds(0, seq_count - 1)
    for send in sends + (o_send,):
        pltpu.make_async_copy(k_all.at[others], k_all.at[others], send).wait()
    kept_others = pl.ds(0, kept_own * (blk_count - 1))
    pltpu.make_async_copy(kept_all.at[kept_others], kept_all.at[kept_others], kept_send).wait()
    pltpu.make_async_copy(out_ref, out_ref, o_recv).wait()


def per_device(qkv, kept_kv, cur_list, kept_list, kept_count):
    seq_count = lax.axis_size("seq")
    blk_count = lax.axis_size("blk")
    tile_len = qkv.shape[0]
    width = HEAD_DIM
    near_count = cur_list.shape[1]
    window = kept_list.shape[1]
    block = (tile_len, width)
    smem = pl.BlockSpec(memory_space=pltpu.SMEM)
    hbm = pl.BlockSpec(memory_space=pl.ANY)
    dma = pltpu.SemaphoreType.DMA
    return pl.pallas_call(
        functools.partial(kernel, seq_count, blk_count),
        out_shape=jax.ShapeDtypeStruct((tile_len, seq_count * width), jnp.bfloat16),
        in_specs=[smem, smem, smem, hbm, hbm],
        out_specs=pl.BlockSpec(memory_space=pltpu.VMEM),
        scratch_shapes=[
            pltpu.VMEM((3, seq_count) + block, jnp.bfloat16),
            pltpu.VMEM((seq_count,) + block, jnp.bfloat16),
            pltpu.VMEM((seq_count,) + block, jnp.bfloat16),
            pltpu.VMEM((seq_count,) + block, jnp.bfloat16),
            pltpu.VMEM((kept_kv.shape[0] * blk_count, 2) + block, jnp.bfloat16),
            pltpu.VMEM((tile_len, (near_count + window) * width), jnp.float32),
            pltpu.VMEM((seq_count, tile_len, near_count * width), jnp.bfloat16),
            pltpu.VMEM((seq_count,) + block, jnp.float32),
            pltpu.VMEM((seq_count,) + block, jnp.float32),
            pltpu.VMEM((seq_count,) + block, jnp.bfloat16),
            dma((3,)),
            dma,
            dma,
            dma,
            dma,
            dma,
            dma((seq_count,)),
            dma,
            dma,
            dma,
            dma,
        ],
        compiler_params=pltpu.CompilerParams(
            collective_id=0, has_side_effects=True, vmem_limit_bytes=50 << 20
        ),
    )(cur_list.T, kept_list.T, kept_count, qkv, kept_kv)


def solution(mesh):
    placed = (P(("seq", "blk"), None), P("blk", None, None, "seq"), P(), P(), P())
    return jax.shard_map(
        per_device, mesh=mesh, in_specs=placed, out_specs=P(("seq", "blk"), None), check_vma=False
    )
```

```python
import functools
import math

import jax
import jax.numpy as jnp
from jax import lax
from jax.experimental import pallas as pl
from jax.experimental.pallas import tpu as pltpu
from jax.sharding import PartitionSpec as P

HEAD_DIM = 128
MASKED_SCORE = -1e30
MESH = pl.DeviceIdType.MESH
LOG2_E = 1.4426950408889634


def kernel(
    seq_count,
    blk_count,
    cur_hbm,
    kept_list_hbm,
    count_hbm,
    qkv_ref,
    kept_ref,
    out_ref,
    cur_ref,
    kept_list_ref,
    count_ref,
    stage,
    q_all,
    k_all,
    v_all,
    kept_all,
    scores,
    mixed,
    list_sem,
    stage_sem,
    kept_send,
    kept_recv,
    k_send,
    k_recv,
    q_send,
    q_recv,
    v_send,
    v_recv,
    o_send,
    o_recv,
):
    me = lax.axis_index("seq")
    region = lax.axis_index("blk")
    near_count = cur_ref.shape[0]
    window = kept_list_ref.shape[0]
    kept_own = kept_ref.shape[0]
    width = HEAD_DIM
    factor = LOG2_E / math.sqrt(width)

    order = (1, 2, 0)

    def stage_copy(slot, group, head):
        column = pl.multiple_of((group * seq_count + head) * width, width)
        return pltpu.make_async_copy(
            qkv_ref.at[:, pl.ds(column, width)], stage.at[slot, head], stage_sem.at[slot]
        )

    for slot, group in enumerate(order):

        @pl.loop(0, seq_count)
        def _(head, slot=slot, group=group):
            stage_copy(slot, group, head).start()

    lists = ((cur_hbm, cur_ref), (kept_list_hbm, kept_list_ref), (count_hbm, count_ref))
    list_copies = [
        pltpu.make_async_copy(source, target, list_sem.at[n])
        for n, (source, target) in enumerate(lists)
    ]
    for copy in list_copies:
        copy.start()

    barrier = pltpu.get_barrier_semaphore()

    @pl.loop(1, seq_count)
    def _(step):
        pl.semaphore_signal(
            barrier, inc=1, device_id={"seq": lax.rem(me + step, seq_count)}, device_id_type=MESH
        )

    @pl.loop(1, blk_count)
    def _(step):
        pl.semaphore_signal(
            barrier, inc=1, device_id={"blk": lax.rem(region + step, blk_count)}, device_id_type=MESH
        )

    pl.semaphore_wait(barrier, seq_count - 1 + blk_count - 1)

    buffers = (k_all, v_all, q_all)
    sends = (k_send, v_send, q_send)
    recvs = (k_recv, v_recv, q_recv)

    def send_group(slot):
        pltpu.make_async_copy(stage.at[slot], stage.at[slot], stage_sem.at[slot]).wait()
        target, send, recv = buffers[slot], sends[slot], recvs[slot]
        recv_mine = recv.at[me] if slot == 2 else recv
        pltpu.make_async_copy(stage.at[slot, me], target.at[me], recv_mine).start()

        @pl.loop(1, seq_count)
        def _(step):
            other = lax.rem(me + step, seq_count)
            pltpu.make_async_remote_copy(
                src_ref=stage.at[slot, other],
                dst_ref=target.at[me],
                send_sem=send,
                recv_sem=recv_mine,
                device_id={"seq": other},
                device_id_type=MESH,
            ).start()

    send_group(0)
    kept_mine = pl.ds(region * kept_own, kept_own)
    pltpu.make_async_copy(kept_ref, kept_all.at[kept_mine], kept_recv).start()

    @pl.loop(1, blk_count)
    def _(step):
        other = lax.rem(region + step, blk_count)
        pltpu.make_async_remote_copy(
            src_ref=kept_ref,
            dst_ref=kept_all.at[kept_mine],
            send_sem=kept_send,
            recv_sem=kept_recv,
            device_id={"blk": other},
            device_id_type=MESH,
        ).start()

    send_group(1)
    send_group(2)

    for copy in list_copies:
        copy.wait()
    pltpu.make_async_copy(k_all, k_all, k_recv).wait()
    pltpu.make_async_copy(kept_all, kept_all, kept_recv).wait()
    pltpu.make_async_copy(v_all, v_all, v_recv).wait()

    columns_mine = pl.ds(pl.multiple_of(me * width, width), width)

    def send_out(tile):
        pltpu.make_async_remote_copy(
            src_ref=mixed.at[tile],
            dst_ref=out_ref.at[:, columns_mine],
            send_sem=o_send,
            recv_sem=o_recv,
            device_id={"seq": tile},
            device_id_type=MESH,
        ).start()

    contract_last = (((1,), (1,)), ((), ()))

    @pl.loop(0, seq_count)
    def _(step):
        tile = lax.rem(me + seq_count - step, seq_count)
        pltpu.make_async_copy(q_all.at[tile], q_all.at[tile], q_recv.at[tile]).wait()
        row = tile * blk_count + region
        queries = q_all[tile]
        live = count_ref[row]
        top = None
        for pair in range((near_count + window) // 2):
            first = 2 * pair
            if first < near_count:
                ids = [cur_ref[first + n, row] // blk_count for n in range(2)]
                keys = [k_all[i] for i in ids]
            else:
                slots = [first - near_count + n for n in range(2)]
                keys = [kept_all[kept_list_ref[w, row], 0] for w in slots]
            product = lax.dot_general(
                queries,
                jnp.concatenate(keys, axis=0),
                contract_last,
                preferred_element_type=jnp.float32,
            )
            for n in range(2):
                part = product[:, n * width : (n + 1) * width]
                if first >= near_count + 1 or (first >= near_count and n > 0):
                    part = part + jnp.where(first - near_count + n < live, 0.0, MASKED_SCORE)
                scores[:, pl.ds((first + n) * width, width)] = part
                top = part if top is None else jnp.maximum(top, part)
        row_max = jnp.max(top, axis=1, keepdims=True)
        total = None
        mixture = None
        for pair in range((near_count + window) // 2):
            first = 2 * pair
            weight = jnp.exp2((scores[:, pl.ds(first * width, 2 * width)] - row_max) * factor)
            half = weight[:, :width] + weight[:, width:]
            total = half if total is None else total + half
            rounded = weight.astype(jnp.bfloat16)
            if first < near_count:
                ids = [cur_ref[first + n, row] // blk_count for n in range(2)]
                values = [v_all[i] for i in ids]
            else:
                slots = [first - near_count + n for n in range(2)]
                values = [kept_all[kept_list_ref[w, row], 1] for w in slots]
            term = jnp.dot(
                rounded, jnp.concatenate(values, axis=0), preferred_element_type=jnp.float32
            )
            mixture = term if mixture is None else mixture + term
        row_total = jnp.sum(total, axis=1, keepdims=True)
        mixed[tile] = (mixture / row_total).astype(jnp.bfloat16)

        @pl.when(step > 1)
        def _():
            send_out(lax.rem(me + seq_count - step + 1, seq_count))

    send_out(lax.rem(me + 1, seq_count))
    own_copy = pltpu.make_async_copy(mixed.at[me], out_ref.at[:, columns_mine], o_recv)
    own_copy.start()

    others = pl.ds(0, seq_count - 1)
    for send in sends + (o_send,):
        pltpu.make_async_copy(k_all.at[others], k_all.at[others], send).wait()
    kept_others = pl.ds(0, kept_own * (blk_count - 1))
    pltpu.make_async_copy(kept_all.at[kept_others], kept_all.at[kept_others], kept_send).wait()
    pltpu.make_async_copy(out_ref, out_ref, o_recv).wait()


def per_device(qkv, kept_kv, cur_list, kept_list, kept_count):
    seq_count = lax.axis_size("seq")
    blk_count = lax.axis_size("blk")
    tile_len = qkv.shape[0]
    width = HEAD_DIM
    near_count = cur_list.shape[1]
    window = kept_list.shape[1]
    block = (tile_len, width)
    hbm = pl.BlockSpec(memory_space=pltpu.HBM)
    dma = pltpu.SemaphoreType.DMA
    return pl.pallas_call(
        functools.partial(kernel, seq_count, blk_count),
        out_shape=jax.ShapeDtypeStruct((tile_len, seq_count * width), jnp.bfloat16),
        in_specs=[hbm] * 5,
        out_specs=pl.BlockSpec(memory_space=pltpu.VMEM),
        scratch_shapes=[
            pltpu.SMEM(cur_list.shape[::-1], jnp.int32),
            pltpu.SMEM(kept_list.shape[::-1], jnp.int32),
            pltpu.SMEM(kept_count.shape, jnp.int32),
            pltpu.VMEM((3, seq_count) + block, jnp.bfloat16),
            pltpu.VMEM((seq_count,) + block, jnp.bfloat16),
            pltpu.VMEM((seq_count,) + block, jnp.bfloat16),
            pltpu.VMEM((seq_count,) + block, jnp.bfloat16),
            pltpu.VMEM((kept_kv.shape[0] * blk_count, 2) + block, jnp.bfloat16),
            pltpu.VMEM((tile_len, (near_count + window) * width), jnp.float32),
            pltpu.VMEM((seq_count,) + block, jnp.bfloat16),
            dma((3,)),
            dma((3,)),
            dma,
            dma,
            dma,
            dma,
            dma,
            dma((seq_count,)),
            dma,
            dma,
            dma,
            dma,
        ],
        compiler_params=pltpu.CompilerParams(
            collective_id=0, has_side_effects=True, vmem_limit_bytes=50 << 20
        ),
    )(*(pltpu.with_memory_space_constraint(a, pltpu.HBM) for a in (cur_list.T, kept_list.T, kept_count, qkv, kept_kv)))


def solution(mesh):
    placed = (P(("seq", "blk"), None), P("blk", None, None, "seq"), P(), P(), P())
    return jax.shard_map(
        per_device, mesh=mesh, in_specs=placed, out_specs=P(("seq", "blk"), None), check_vma=False
    )
```

```python
import functools
import math

import jax
import jax.numpy as jnp
from jax import lax
from jax.experimental import pallas as pl
from jax.experimental.pallas import tpu as pltpu
from jax.sharding import PartitionSpec as P

HEAD_DIM = 128
MASKED_SCORE = -1e30
MESH = pl.DeviceIdType.MESH
LOG2_E = 1.4426950408889634


def kernel(
    seq_count,
    blk_count,
    rows,
    cur_hbm,
    kept_list_hbm,
    count_hbm,
    qkv_ref,
    kept_ref,
    out_ref,
    cur_ref,
    kept_list_ref,
    count_ref,
    stage,
    q_all,
    k_all,
    v_all,
    kept_all,
    scores,
    mixed,
    list_sem,
    stage_sem,
    kept_send,
    kept_recv,
    k_send,
    k_recv,
    q_send,
    q_recv,
    v_send,
    v_recv,
    o_send,
    o_recv,
):
    me = lax.axis_index("seq")
    rings = seq_count // rows
    my_z = me // rows
    my_x = lax.rem(me, rows)

    def partner(step, back):
        turn = lax.rem(step, rings)
        far = (turn + 1) // 2 * (1 - 2 * lax.rem(turn, 2)) + rings // 2
        side = lax.rem(step // rings + 1, rows)
        if back:
            far, side = rings - far, rows - side
        return lax.rem(my_z + far, rings) * rows + lax.rem(my_x + side, rows)

    region = lax.axis_index("blk")
    near_count = cur_ref.shape[0]
    window = kept_list_ref.shape[0]
    kept_own = kept_ref.shape[0]
    width = HEAD_DIM
    factor = LOG2_E / math.sqrt(width)

    barrier = pltpu.get_barrier_semaphore()

    @pl.loop(0, seq_count - 1)
    def _(step):
        pl.semaphore_signal(
            barrier, inc=1, device_id={"seq": partner(step, False)}, device_id_type=MESH
        )

    @pl.loop(1, blk_count)
    def _(step):
        pl.semaphore_signal(
            barrier, inc=1, device_id={"blk": lax.rem(region + step, blk_count)}, device_id_type=MESH
        )

    order = (1, 2, 0)

    def stage_copy(slot, group, head):
        column = pl.multiple_of((group * seq_count + head) * width, width)
        return pltpu.make_async_copy(
            qkv_ref.at[:, pl.ds(column, width)], stage.at[slot, head], stage_sem.at[slot]
        )

    for slot, group in enumerate(order):

        @pl.loop(0, seq_count)
        def _(head, slot=slot, group=group):
            stage_copy(slot, group, head).start()

    lists = ((cur_hbm, cur_ref), (kept_list_hbm, kept_list_ref), (count_hbm, count_ref))
    list_copies = [
        pltpu.make_async_copy(source, target, list_sem.at[n])
        for n, (source, target) in enumerate(lists)
    ]
    for copy in list_copies:
        copy.start()

    pl.semaphore_wait(barrier, seq_count - 1 + blk_count - 1)

    buffers = (k_all, v_all, q_all)
    sends = (k_send, v_send, q_send)
    recvs = (k_recv, v_recv, q_recv)

    def send_group(slot):
        pltpu.make_async_copy(stage.at[slot], stage.at[slot], stage_sem.at[slot]).wait()
        target, send, recv = buffers[slot], sends[slot], recvs[slot]
        recv_mine = recv.at[me] if slot == 2 else recv
        pltpu.make_async_copy(stage.at[slot, me], target.at[me], recv_mine).start()

        @pl.loop(0, seq_count - 1)
        def _(step):
            other = partner(step, False)
            pltpu.make_async_remote_copy(
                src_ref=stage.at[slot, other],
                dst_ref=target.at[me],
                send_sem=send,
                recv_sem=recv_mine,
                device_id={"seq": other},
                device_id_type=MESH,
            ).start()

    send_group(0)
    kept_mine = pl.ds(region * kept_own, kept_own)
    pltpu.make_async_copy(kept_ref, kept_all.at[kept_mine], kept_recv).start()

    @pl.loop(1, blk_count)
    def _(step):
        other = lax.rem(region + step, blk_count)
        pltpu.make_async_remote_copy(
            src_ref=kept_ref,
            dst_ref=kept_all.at[kept_mine],
            send_sem=kept_send,
            recv_sem=kept_recv,
            device_id={"blk": other},
            device_id_type=MESH,
        ).start()

    send_group(1)
    send_group(2)

    for copy in list_copies:
        copy.wait()
    pltpu.make_async_copy(k_all, k_all, k_recv).wait()
    pltpu.make_async_copy(kept_all, kept_all, kept_recv).wait()
    pltpu.make_async_copy(v_all, v_all, v_recv).wait()

    columns_mine = pl.ds(pl.multiple_of(me * width, width), width)

    def send_out(tile):
        pltpu.make_async_remote_copy(
            src_ref=mixed.at[tile],
            dst_ref=out_ref.at[:, columns_mine],
            send_sem=o_send,
            recv_sem=o_recv,
            device_id={"seq": tile},
            device_id_type=MESH,
        ).start()

    contract_last = (((1,), (1,)), ((), ()))

    @pl.loop(0, seq_count)
    def _(step):
        tile = partner(step, True)
        pltpu.make_async_copy(q_all.at[tile], q_all.at[tile], q_recv.at[tile]).wait()
        row = tile * blk_count + region
        queries = q_all[tile]
        live = count_ref[row]
        top = None
        for pair in range((near_count + window) // 2):
            first = 2 * pair
            if first < near_count:
                ids = [cur_ref[first + n, row] // blk_count for n in range(2)]
                keys = [k_all[i] for i in ids]
            else:
                slots = [first - near_count + n for n in range(2)]
                keys = [kept_all[kept_list_ref[w, row], 0] for w in slots]
            product = lax.dot_general(
                queries,
                jnp.concatenate(keys, axis=0),
                contract_last,
                preferred_element_type=jnp.float32,
            )
            for n in range(2):
                part = product[:, n * width : (n + 1) * width]
                if first >= near_count + 1 or (first >= near_count and n > 0):
                    part = part + jnp.where(first - near_count + n < live, 0.0, MASKED_SCORE)
                scores[:, pl.ds((first + n) * width, width)] = part
                top = part if top is None else jnp.maximum(top, part)
        row_max = jnp.max(top, axis=1, keepdims=True)
        total = None
        mixture = None
        for pair in range((near_count + window) // 2):
            first = 2 * pair
            weight = jnp.exp2((scores[:, pl.ds(first * width, 2 * width)] - row_max) * factor)
            half = weight[:, :width] + weight[:, width:]
            total = half if total is None else total + half
            rounded = weight.astype(jnp.bfloat16)
            if first < near_count:
                ids = [cur_ref[first + n, row] // blk_count for n in range(2)]
                values = [v_all[i] for i in ids]
            else:
                slots = [first - near_count + n for n in range(2)]
                values = [kept_all[kept_list_ref[w, row], 1] for w in slots]
            term = jnp.dot(
                rounded, jnp.concatenate(values, axis=0), preferred_element_type=jnp.float32
            )
            mixture = term if mixture is None else mixture + term
        row_total = jnp.sum(total, axis=1, keepdims=True)
        mixed[tile] = (mixture / row_total).astype(jnp.bfloat16)

        @pl.when(step > 0)
        def _():
            send_out(partner(step - 1, True))

    own_copy = pltpu.make_async_copy(mixed.at[me], out_ref.at[:, columns_mine], o_recv)
    own_copy.start()

    others = pl.ds(0, seq_count - 1)
    for send in sends + (o_send,):
        pltpu.make_async_copy(k_all.at[others], k_all.at[others], send).wait()
    kept_others = pl.ds(0, kept_own * (blk_count - 1))
    pltpu.make_async_copy(kept_all.at[kept_others], kept_all.at[kept_others], kept_send).wait()
    pltpu.make_async_copy(out_ref, out_ref, o_recv).wait()


def per_device(qkv, kept_kv, cur_list, kept_list, kept_count):
    seq_count = lax.axis_size("seq")
    blk_count = lax.axis_size("blk")
    tile_len = qkv.shape[0]
    width = HEAD_DIM
    near_count = cur_list.shape[1]
    window = kept_list.shape[1]
    block = (tile_len, width)
    hbm = pl.BlockSpec(memory_space=pltpu.HBM)
    dma = pltpu.SemaphoreType.DMA
    return pl.pallas_call(
        functools.partial(kernel, seq_count, blk_count, 4),
        out_shape=jax.ShapeDtypeStruct((tile_len, seq_count * width), jnp.bfloat16),
        in_specs=[hbm] * 5,
        out_specs=pl.BlockSpec(memory_space=pltpu.VMEM),
        scratch_shapes=[
            pltpu.SMEM(cur_list.shape[::-1], jnp.int32),
            pltpu.SMEM(kept_list.shape[::-1], jnp.int32),
            pltpu.SMEM(kept_count.shape, jnp.int32),
            pltpu.VMEM((3, seq_count) + block, jnp.bfloat16),
            pltpu.VMEM((seq_count,) + block, jnp.bfloat16),
            pltpu.VMEM((seq_count,) + block, jnp.bfloat16),
            pltpu.VMEM((seq_count,) + block, jnp.bfloat16),
            pltpu.VMEM((kept_kv.shape[0] * blk_count, 2) + block, jnp.bfloat16),
            pltpu.VMEM((tile_len, (near_count + window) * width), jnp.float32),
            pltpu.VMEM((seq_count,) + block, jnp.bfloat16),
            dma((3,)),
            dma((3,)),
            dma,
            dma,
            dma,
            dma,
            dma,
            dma((seq_count,)),
            dma,
            dma,
            dma,
            dma,
        ],
        compiler_params=pltpu.CompilerParams(
            collective_id=0, has_side_effects=True, vmem_limit_bytes=50 << 20
        ),
    )(*(pltpu.with_memory_space_constraint(a, pltpu.HBM) for a in (cur_list.T, kept_list.T, kept_count, qkv, kept_kv)))


def solution(mesh):
    placed = (P(("seq", "blk"), None), P("blk", None, None, "seq"), P(), P(), P())
    return jax.shard_map(
        per_device, mesh=mesh, in_specs=placed, out_specs=P(("seq", "blk"), None), check_vma=False
    )
```

```python
import functools
import math

import jax
import jax.numpy as jnp
from jax import lax
from jax.experimental import pallas as pl
from jax.experimental.pallas import tpu as pltpu
from jax.sharding import PartitionSpec as P

HEAD_DIM = 128
MASKED_SCORE = -1e30
MESH = pl.DeviceIdType.MESH
LOG2_E = 1.4426950408889634


def kernel(
    seq_count,
    blk_count,
    rows,
    cur_hbm,
    kept_list_hbm,
    count_hbm,
    qkv_ref,
    kept_ref,
    out_ref,
    cur_ref,
    kept_list_ref,
    count_ref,
    stage,
    q_all,
    k_all,
    v_all,
    kept_all,
    scores,
    mixed,
    list_sem,
    stage_sem,
    kept_send,
    kept_recv,
    k_send,
    k_recv,
    q_send,
    q_recv,
    v_send,
    v_recv,
    o_send,
    o_recv,
    level_sem,
):
    me = lax.axis_index("seq")
    rings = seq_count // rows
    my_z = me // rows
    my_x = lax.rem(me, rows)

    z_at = [lax.rem(my_z + far, rings) for far in range(rings)]
    x_at = [lax.rem(my_x + side, rows) for side in range(rows)]

    def place(far, side):
        return z_at[far] * rows + x_at[side]

    def hops(far, side):
        return min(far, rings - far) + min(side, rows - side)

    turns = [rings // 2]
    for far in range(rings // 2 - 1, 0, -1):
        turns += [far, rings - far]
    turns += [0]
    partners = [(far, side % rows) for side in range(1, rows + 1) for far in turns]
    partners.remove((0, 0))
    reach = rings // 2 + rows // 2
    neighbours = [place(far, side) for far, side in partners if hops(far, side) == 1]

    def source(step):
        turn = lax.rem(step, rings)
        far = (turn + 1) // 2 * (1 - 2 * lax.rem(turn, 2)) + rings // 2
        side = lax.rem(step // rings + 1, rows)
        return lax.rem(my_z + far, rings) * rows + lax.rem(my_x + rows - side, rows)

    region = lax.axis_index("blk")
    near_count = cur_ref.shape[0]
    window = kept_list_ref.shape[0]
    kept_own = kept_ref.shape[0]
    width = HEAD_DIM
    factor = LOG2_E / math.sqrt(width)

    barrier = pltpu.get_barrier_semaphore()

    for neighbour in neighbours:
        pl.semaphore_signal(barrier, inc=1, device_id={"seq": neighbour}, device_id_type=MESH)

    @pl.loop(1, blk_count)
    def _(step):
        pl.semaphore_signal(
            barrier, inc=1, device_id={"blk": lax.rem(region + step, blk_count)}, device_id_type=MESH
        )

    order = (1, 2, 0)

    def stage_copy(slot, group, head):
        column = pl.multiple_of((group * seq_count + head) * width, width)
        return pltpu.make_async_copy(
            qkv_ref.at[:, pl.ds(column, width)], stage.at[slot, head], stage_sem.at[slot]
        )

    for slot, group in enumerate(order):

        @pl.loop(0, seq_count)
        def _(head, slot=slot, group=group):
            stage_copy(slot, group, head).start()

    lists = ((cur_hbm, cur_ref), (kept_list_hbm, kept_list_ref), (count_hbm, count_ref))
    list_copies = [
        pltpu.make_async_copy(source, target, list_sem.at[n])
        for n, (source, target) in enumerate(lists)
    ]
    for copy in list_copies:
        copy.start()

    for slot in range(3):
        pltpu.make_async_copy(stage.at[slot], stage.at[slot], stage_sem.at[slot]).wait()

    pl.semaphore_wait(barrier, len(neighbours) + blk_count - 1)

    def tell(level):
        for neighbour in neighbours:
            pl.semaphore_signal(
                level_sem.at[level], inc=1, device_id={"seq": neighbour}, device_id_type=MESH
            )

    tell(0)

    buffers = (k_all, v_all, q_all)
    sends = (k_send, v_send, q_send)
    recvs = (k_recv, v_recv, q_recv)

    def send_group(slot, nearest, farthest):
        target, send, recv = buffers[slot], sends[slot], recvs[slot]
        recv_mine = recv.at[me] if slot == 2 else recv

        for far, side in partners:
            if nearest <= hops(far, side) <= farthest:
                other = place(far, side)
                pltpu.make_async_remote_copy(
                    src_ref=stage.at[slot, other],
                    dst_ref=target.at[me],
                    send_sem=send,
                    recv_sem=recv_mine,
                    device_id={"seq": other},
                    device_id_type=MESH,
                ).start()

    send_group(0, 1, 1)
    send_group(1, 1, 1)

    pl.semaphore_wait(level_sem.at[0], len(neighbours))
    tell(1)
    send_group(0, 2, 2)
    send_group(1, 2, 2)

    kept_mine = pl.ds(region * kept_own, kept_own)

    @pl.loop(1, blk_count)
    def _(step):
        other = lax.rem(region + step, blk_count)
        pltpu.make_async_remote_copy(
            src_ref=kept_ref,
            dst_ref=kept_all.at[kept_mine],
            send_sem=kept_send,
            recv_sem=kept_recv,
            device_id={"blk": other},
            device_id_type=MESH,
        ).start()

    pltpu.make_async_copy(kept_ref, kept_all.at[kept_mine], kept_recv).start()
    for slot in range(3):
        recv = recvs[slot].at[me] if slot == 2 else recvs[slot]
        pltpu.make_async_copy(stage.at[slot, me], buffers[slot].at[me], recv).start()

    for level in range(1, reach - 1):
        pl.semaphore_wait(level_sem.at[level], len(neighbours))
        if level < reach - 2:
            tell(level + 1)
        send_group(0, level + 2, level + 2)
        send_group(1, level + 2, level + 2)

    send_group(2, 1, reach)

    for copy in list_copies:
        copy.wait()
    pltpu.make_async_copy(k_all, k_all, k_recv).wait()
    pltpu.make_async_copy(kept_all, kept_all, kept_recv).wait()
    pltpu.make_async_copy(v_all, v_all, v_recv).wait()

    columns_mine = pl.ds(pl.multiple_of(me * width, width), width)

    def send_out(tile):
        pltpu.make_async_remote_copy(
            src_ref=mixed.at[tile],
            dst_ref=out_ref.at[:, columns_mine],
            send_sem=o_send,
            recv_sem=o_recv,
            device_id={"seq": tile},
            device_id_type=MESH,
        ).start()

    contract_last = (((1,), (1,)), ((), ()))

    @pl.loop(0, seq_count)
    def _(step):
        tile = source(step)
        pltpu.make_async_copy(q_all.at[tile], q_all.at[tile], q_recv.at[tile]).wait()
        row = tile * blk_count + region
        queries = q_all[tile]
        live = count_ref[row]
        top = None
        for pair in range((near_count + window) // 2):
            first = 2 * pair
            if first < near_count:
                ids = [cur_ref[first + n, row] // blk_count for n in range(2)]
                keys = [k_all[i] for i in ids]
            else:
                slots = [first - near_count + n for n in range(2)]
                keys = [kept_all[kept_list_ref[w, row], 0] for w in slots]
            product = lax.dot_general(
                queries,
                jnp.concatenate(keys, axis=0),
                contract_last,
                preferred_element_type=jnp.float32,
            )
            for n in range(2):
                part = product[:, n * width : (n + 1) * width]
                if first >= near_count + 1 or (first >= near_count and n > 0):
                    part = part + jnp.where(first - near_count + n < live, 0.0, MASKED_SCORE)
                scores[:, pl.ds((first + n) * width, width)] = part
                top = part if top is None else jnp.maximum(top, part)
        row_max = jnp.max(top, axis=1, keepdims=True)
        total = None
        mixture = None
        for pair in range((near_count + window) // 2):
            first = 2 * pair
            weight = jnp.exp2((scores[:, pl.ds(first * width, 2 * width)] - row_max) * factor)
            half = weight[:, :width] + weight[:, width:]
            total = half if total is None else total + half
            rounded = weight.astype(jnp.bfloat16)
            if first < near_count:
                ids = [cur_ref[first + n, row] // blk_count for n in range(2)]
                values = [v_all[i] for i in ids]
            else:
                slots = [first - near_count + n for n in range(2)]
                values = [kept_all[kept_list_ref[w, row], 1] for w in slots]
            term = jnp.dot(
                rounded, jnp.concatenate(values, axis=0), preferred_element_type=jnp.float32
            )
            mixture = term if mixture is None else mixture + term
        row_total = jnp.sum(total, axis=1, keepdims=True)
        mixed[tile] = (mixture / row_total).astype(jnp.bfloat16)

        @pl.when(step > 0)
        def _():
            send_out(source(step - 1))

    own_copy = pltpu.make_async_copy(mixed.at[me], out_ref.at[:, columns_mine], o_recv)
    own_copy.start()

    others = pl.ds(0, seq_count - 1)
    for send in sends + (o_send,):
        pltpu.make_async_copy(k_all.at[others], k_all.at[others], send).wait()
    kept_others = pl.ds(0, kept_own * (blk_count - 1))
    pltpu.make_async_copy(kept_all.at[kept_others], kept_all.at[kept_others], kept_send).wait()
    pltpu.make_async_copy(out_ref, out_ref, o_recv).wait()


def per_device(qkv, kept_kv, cur_list, kept_list, kept_count):
    seq_count = lax.axis_size("seq")
    blk_count = lax.axis_size("blk")
    tile_len = qkv.shape[0]
    width = HEAD_DIM
    near_count = cur_list.shape[1]
    window = kept_list.shape[1]
    block = (tile_len, width)
    hbm = pl.BlockSpec(memory_space=pltpu.HBM)
    dma = pltpu.SemaphoreType.DMA
    return pl.pallas_call(
        functools.partial(kernel, seq_count, blk_count, 4),
        out_shape=jax.ShapeDtypeStruct((tile_len, seq_count * width), jnp.bfloat16),
        in_specs=[hbm] * 5,
        out_specs=pl.BlockSpec(memory_space=pltpu.VMEM),
        scratch_shapes=[
            pltpu.SMEM(cur_list.shape[::-1], jnp.int32),
            pltpu.SMEM(kept_list.shape[::-1], jnp.int32),
            pltpu.SMEM(kept_count.shape, jnp.int32),
            pltpu.VMEM((3, seq_count) + block, jnp.bfloat16),
            pltpu.VMEM((seq_count,) + block, jnp.bfloat16),
            pltpu.VMEM((seq_count,) + block, jnp.bfloat16),
            pltpu.VMEM((seq_count,) + block, jnp.bfloat16),
            pltpu.VMEM((kept_kv.shape[0] * blk_count, 2) + block, jnp.bfloat16),
            pltpu.VMEM((tile_len, (near_count + window) * width), jnp.float32),
            pltpu.VMEM((seq_count,) + block, jnp.bfloat16),
            dma((3,)),
            dma((3,)),
            dma,
            dma,
            dma,
            dma,
            dma,
            dma((seq_count,)),
            dma,
            dma,
            dma,
            dma,
            pltpu.SemaphoreType.REGULAR((seq_count // 8 + 1,)),
        ],
        compiler_params=pltpu.CompilerParams(
            collective_id=0, has_side_effects=True, vmem_limit_bytes=50 << 20
        ),
    )(*(pltpu.with_memory_space_constraint(a, pltpu.HBM) for a in (cur_list.T, kept_list.T, kept_count, qkv, kept_kv)))


def solution(mesh):
    placed = (P(("seq", "blk"), None), P("blk", None, None, "seq"), P(), P(), P())
    return jax.shard_map(
        per_device, mesh=mesh, in_specs=placed, out_specs=P(("seq", "blk"), None), check_vma=False
    )
```

```python
import functools
import math

import jax
import jax.numpy as jnp
from jax import lax
from jax.experimental import pallas as pl
from jax.experimental.pallas import tpu as pltpu
from jax.sharding import PartitionSpec as P

HEAD_DIM = 128
MASKED_SCORE = -1e30
MESH = pl.DeviceIdType.MESH
LOG2_E = 1.4426950408889634


def kernel(
    seq_count,
    blk_count,
    rows,
    cores,
    cur_hbm,
    kept_list_hbm,
    count_hbm,
    qkv_ref,
    kept_ref,
    out_ref,
    cur_ref,
    kept_list_ref,
    count_ref,
    stage,
    q_all,
    k_all,
    v_all,
    kept_all,
    scores,
    mixed,
    list_sem,
    stage_sem,
    kept_send,
    kept_recv,
    k_send,
    k_recv,
    q_send,
    q_recv,
    v_send,
    v_recv,
    o_send,
    o_recv,
    level_sem,
    blk_sem,
):
    me = lax.axis_index("seq")
    rings = seq_count // rows
    my_z = me // rows
    my_x = lax.rem(me, rows)

    z_at = [lax.rem(my_z + far, rings) for far in range(rings)]
    x_at = [lax.rem(my_x + side, rows) for side in range(rows)]

    def place(far, side):
        return z_at[far] * rows + x_at[side]

    def hops(far, side):
        return min(far, rings - far) + min(side, rows - side)

    turns = [rings // 2]
    for far in range(rings // 2 - 1, 0, -1):
        turns += [far, rings - far]
    turns += [0]
    partners = [(far, side % rows) for side in range(1, rows + 1) for far in turns]
    partners.remove((0, 0))
    reach = rings // 2 + rows // 2
    neighbours = [place(far, side) for far, side in partners if hops(far, side) == 1]

    def source(step):
        turn = lax.rem(step, rings)
        far = (turn + 1) // 2 * (1 - 2 * lax.rem(turn, 2)) + rings // 2
        side = lax.rem(step // rings + 1, rows)
        return lax.rem(my_z + far, rings) * rows + lax.rem(my_x + rows - side, rows)

    region = lax.axis_index("blk")
    my_y = region // cores
    my_core = lax.rem(region, cores)
    columns = blk_count // cores

    def blk_place(along, core):
        return lax.rem(my_y + along, columns) * cores + lax.rem(my_core + core, cores)

    blk_partners = [(along, core) for core in range(cores) for along in range(columns)]
    blk_partners.remove((0, 0))
    blk_neighbours = [blk_place(*at) for at in ((1, 0), (columns - 1, 0), (0, 1))]
    near_count = cur_ref.shape[0]
    window = kept_list_ref.shape[0]
    kept_own = kept_ref.shape[0]
    width = HEAD_DIM
    factor = LOG2_E / math.sqrt(width)

    barrier = pltpu.get_barrier_semaphore()

    for neighbour in neighbours:
        pl.semaphore_signal(barrier, inc=1, device_id={"seq": neighbour}, device_id_type=MESH)

    for neighbour in blk_neighbours:
        pl.semaphore_signal(barrier, inc=1, device_id={"blk": neighbour}, device_id_type=MESH)

    order = (1, 2, 0)

    def stage_copy(slot, group, head):
        column = pl.multiple_of((group * seq_count + head) * width, width)
        return pltpu.make_async_copy(
            qkv_ref.at[:, pl.ds(column, width)], stage.at[slot, head], stage_sem.at[slot]
        )

    for slot, group in enumerate(order):

        @pl.loop(0, seq_count)
        def _(head, slot=slot, group=group):
            stage_copy(slot, group, head).start()

    lists = ((cur_hbm, cur_ref), (kept_list_hbm, kept_list_ref), (count_hbm, count_ref))
    list_copies = [
        pltpu.make_async_copy(source, target, list_sem.at[n])
        for n, (source, target) in enumerate(lists)
    ]
    for copy in list_copies:
        copy.start()

    pl.semaphore_wait(barrier, len(neighbours) + len(blk_neighbours))

    def tell(level):
        for neighbour in neighbours:
            pl.semaphore_signal(
                level_sem.at[level], inc=1, device_id={"seq": neighbour}, device_id_type=MESH
            )

    def tell_blk(level):
        for neighbour in blk_neighbours:
            pl.semaphore_signal(
                blk_sem.at[level], inc=1, device_id={"blk": neighbour}, device_id_type=MESH
            )

    def staged(slot):
        pltpu.make_async_copy(stage.at[slot], stage.at[slot], stage_sem.at[slot]).wait()

    tell(0)
    tell_blk(0)

    buffers = (k_all, v_all, q_all)
    sends = (k_send, v_send, q_send)
    recvs = (k_recv, v_recv, q_recv)

    def send_group(slot, nearest, farthest):
        target, send, recv = buffers[slot], sends[slot], recvs[slot]
        recv_mine = recv.at[me] if slot == 2 else recv

        for far, side in partners:
            if nearest <= hops(far, side) <= farthest:
                other = place(far, side)
                pltpu.make_async_remote_copy(
                    src_ref=stage.at[slot, other],
                    dst_ref=target.at[me],
                    send_sem=send,
                    recv_sem=recv_mine,
                    device_id={"seq": other},
                    device_id_type=MESH,
                ).start()

    staged(0)
    send_group(0, 1, 1)
    staged(1)
    send_group(1, 1, 1)

    pl.semaphore_wait(level_sem.at[0], len(neighbours))
    tell(1)
    send_group(0, 2, 2)
    pl.semaphore_wait(blk_sem.at[0], len(blk_neighbours))
    tell_blk(1)
    send_group(1, 2, 2)
    staged(2)

    kept_mine = pl.ds(region * kept_own, kept_own)

    pltpu.make_async_copy(kept_ref, kept_all.at[kept_mine], kept_recv).start()
    for slot in range(3):
        recv = recvs[slot].at[me] if slot == 2 else recvs[slot]
        pltpu.make_async_copy(stage.at[slot, me], buffers[slot].at[me], recv).start()

    for level in range(1, reach - 1):
        pl.semaphore_wait(level_sem.at[level], len(neighbours))
        if level < reach - 2:
            tell(level + 1)
        send_group(0, level + 2, level + 2)
        send_group(1, level + 2, level + 2)

    pl.semaphore_wait(blk_sem.at[1], len(blk_neighbours))
    for along, core in blk_partners:
        pltpu.make_async_remote_copy(
            src_ref=kept_ref,
            dst_ref=kept_all.at[kept_mine],
            send_sem=kept_send,
            recv_sem=kept_recv,
            device_id={"blk": blk_place(along, core)},
            device_id_type=MESH,
        ).start()

    send_group(2, 1, reach)

    for copy in list_copies:
        copy.wait()
    pltpu.make_async_copy(k_all, k_all, k_recv).wait()
    pltpu.make_async_copy(kept_all, kept_all, kept_recv).wait()
    pltpu.make_async_copy(v_all, v_all, v_recv).wait()

    columns_mine = pl.ds(pl.multiple_of(me * width, width), width)

    def send_out(tile):
        pltpu.make_async_remote_copy(
            src_ref=mixed.at[tile],
            dst_ref=out_ref.at[:, columns_mine],
            send_sem=o_send,
            recv_sem=o_recv,
            device_id={"seq": tile},
            device_id_type=MESH,
        ).start()

    contract_last = (((1,), (1,)), ((), ()))

    @pl.loop(0, seq_count)
    def _(step):
        tile = source(step)
        pltpu.make_async_copy(q_all.at[tile], q_all.at[tile], q_recv.at[tile]).wait()
        row = tile * blk_count + region
        queries = q_all[tile]
        live = count_ref[row]
        top = None
        for pair in range((near_count + window) // 2):
            first = 2 * pair
            if first < near_count:
                ids = [cur_ref[first + n, row] // blk_count for n in range(2)]
                keys = [k_all[i] for i in ids]
            else:
                slots = [first - near_count + n for n in range(2)]
                keys = [kept_all[kept_list_ref[w, row], 0] for w in slots]
            product = lax.dot_general(
                queries,
                jnp.concatenate(keys, axis=0),
                contract_last,
                preferred_element_type=jnp.float32,
            )
            for n in range(2):
                part = product[:, n * width : (n + 1) * width]
                if first >= near_count + 1 or (first >= near_count and n > 0):
                    part = part + jnp.where(first - near_count + n < live, 0.0, MASKED_SCORE)
                scores[:, pl.ds((first + n) * width, width)] = part
                top = part if top is None else jnp.maximum(top, part)
        row_max = jnp.max(top, axis=1, keepdims=True)
        total = None
        mixture = None
        for pair in range((near_count + window) // 2):
            first = 2 * pair
            weight = jnp.exp2((scores[:, pl.ds(first * width, 2 * width)] - row_max) * factor)
            half = weight[:, :width] + weight[:, width:]
            total = half if total is None else total + half
            rounded = weight.astype(jnp.bfloat16)
            if first < near_count:
                ids = [cur_ref[first + n, row] // blk_count for n in range(2)]
                values = [v_all[i] for i in ids]
            else:
                slots = [first - near_count + n for n in range(2)]
                values = [kept_all[kept_list_ref[w, row], 1] for w in slots]
            term = jnp.dot(
                rounded, jnp.concatenate(values, axis=0), preferred_element_type=jnp.float32
            )
            mixture = term if mixture is None else mixture + term
        row_total = jnp.sum(total, axis=1, keepdims=True)
        mixed[tile] = (mixture / row_total).astype(jnp.bfloat16)

        @pl.when(step > 0)
        def _():
            send_out(source(step - 1))

    own_copy = pltpu.make_async_copy(mixed.at[me], out_ref.at[:, columns_mine], o_recv)
    own_copy.start()

    others = pl.ds(0, seq_count - 1)
    for send in sends + (o_send,):
        pltpu.make_async_copy(k_all.at[others], k_all.at[others], send).wait()
    kept_others = pl.ds(0, kept_own * (blk_count - 1))
    pltpu.make_async_copy(kept_all.at[kept_others], kept_all.at[kept_others], kept_send).wait()
    pltpu.make_async_copy(out_ref, out_ref, o_recv).wait()


def per_device(qkv, kept_kv, cur_list, kept_list, kept_count):
    seq_count = lax.axis_size("seq")
    blk_count = lax.axis_size("blk")
    tile_len = qkv.shape[0]
    width = HEAD_DIM
    near_count = cur_list.shape[1]
    window = kept_list.shape[1]
    block = (tile_len, width)
    hbm = pl.BlockSpec(memory_space=pltpu.HBM)
    dma = pltpu.SemaphoreType.DMA
    return pl.pallas_call(
        functools.partial(kernel, seq_count, blk_count, 4, 2),
        out_shape=jax.ShapeDtypeStruct((tile_len, seq_count * width), jnp.bfloat16),
        in_specs=[hbm] * 5,
        out_specs=pl.BlockSpec(memory_space=pltpu.VMEM),
        scratch_shapes=[
            pltpu.SMEM(cur_list.shape[::-1], jnp.int32),
            pltpu.SMEM(kept_list.shape[::-1], jnp.int32),
            pltpu.SMEM(kept_count.shape, jnp.int32),
            pltpu.VMEM((3, seq_count) + block, jnp.bfloat16),
            pltpu.VMEM((seq_count,) + block, jnp.bfloat16),
            pltpu.VMEM((seq_count,) + block, jnp.bfloat16),
            pltpu.VMEM((seq_count,) + block, jnp.bfloat16),
            pltpu.VMEM((kept_kv.shape[0] * blk_count, 2) + block, jnp.bfloat16),
            pltpu.VMEM((tile_len, (near_count + window) * width), jnp.float32),
            pltpu.VMEM((seq_count,) + block, jnp.bfloat16),
            dma((3,)),
            dma((3,)),
            dma,
            dma,
            dma,
            dma,
            dma,
            dma((seq_count,)),
            dma,
            dma,
            dma,
            dma,
            pltpu.SemaphoreType.REGULAR((seq_count // 8 + 1,)),
            pltpu.SemaphoreType.REGULAR((2,)),
        ],
        compiler_params=pltpu.CompilerParams(
            collective_id=0, has_side_effects=True, vmem_limit_bytes=50 << 20
        ),
    )(*(pltpu.with_memory_space_constraint(a, pltpu.HBM) for a in (cur_list.T, kept_list.T, kept_count, qkv, kept_kv)))


def solution(mesh):
    placed = (P(("seq", "blk"), None), P("blk", None, None, "seq"), P(), P(), P())
    return jax.shard_map(
        per_device, mesh=mesh, in_specs=placed, out_specs=P(("seq", "blk"), None), check_vma=False
    )
```

```python
import functools
import math

import jax
import jax.numpy as jnp
from jax import lax
from jax.experimental import pallas as pl
from jax.experimental.pallas import tpu as pltpu
from jax.sharding import PartitionSpec as P

HEAD_DIM = 128
MASKED_SCORE = -1e30
MESH = pl.DeviceIdType.MESH
LOG2_E = 1.4426950408889634


def kernel(
    seq_count,
    blk_count,
    rows,
    cores,
    cur_hbm,
    kept_list_hbm,
    count_hbm,
    qkv_ref,
    kept_ref,
    out_ref,
    cur_ref,
    kept_list_ref,
    count_ref,
    q_all,
    kv_all,
    kept_all,
    scores,
    mixed,
    list_sem,
    kept_send,
    kept_recv,
    kv_send,
    kv_recv,
    q_send,
    q_recv,
    o_send,
    o_recv,
    level_sem,
    blk_sem,
):
    me = lax.axis_index("seq")
    rings = seq_count // rows
    my_z = me // rows
    my_x = lax.rem(me, rows)

    z_at = [lax.rem(my_z + far, rings) for far in range(rings)]
    x_at = [lax.rem(my_x + side, rows) for side in range(rows)]

    def place(far, side):
        return z_at[far] * rows + x_at[side]

    def hops(far, side):
        return min(far, rings - far) + min(side, rows - side)

    turns = [rings // 2]
    for far in range(rings // 2 - 1, 0, -1):
        turns += [far, rings - far]
    turns += [0]
    partners = [(far, side % rows) for side in range(1, rows + 1) for far in turns]
    partners.remove((0, 0))
    reach = rings // 2 + rows // 2
    neighbours = [place(far, side) for far, side in partners if hops(far, side) == 1]

    def partner(step, back):
        turn = lax.rem(step, rings)
        far = (turn + 1) // 2 * (1 - 2 * lax.rem(turn, 2)) + rings // 2
        side = lax.rem(step // rings + 1, rows)
        if back:
            far, side = rings - far, rows - side
        return lax.rem(my_z + far, rings) * rows + lax.rem(my_x + side, rows)

    region = lax.axis_index("blk")
    my_y = region // cores
    my_core = lax.rem(region, cores)
    columns = blk_count // cores

    def blk_place(along, core):
        return lax.rem(my_y + along, columns) * cores + lax.rem(my_core + core, cores)

    blk_partners = [(along, core) for core in range(cores) for along in range(columns)]
    blk_partners.remove((0, 0))
    blk_neighbours = [blk_place(*at) for at in ((1, 0), (columns - 1, 0), (0, 1))]
    near_count = cur_ref.shape[0]
    window = kept_list_ref.shape[0]
    kept_own = kept_ref.shape[0]
    width = HEAD_DIM
    factor = LOG2_E / math.sqrt(width)

    barrier = pltpu.get_barrier_semaphore()

    for neighbour in neighbours:
        pl.semaphore_signal(barrier, inc=1, device_id={"seq": neighbour}, device_id_type=MESH)

    for neighbour in blk_neighbours:
        pl.semaphore_signal(barrier, inc=1, device_id={"blk": neighbour}, device_id_type=MESH)

    def own_block(group, head):
        column = pl.multiple_of((group * seq_count + head) * width, width)
        return qkv_ref.at[:, pl.ds(column, width)]

    lists = ((cur_hbm, cur_ref), (kept_list_hbm, kept_list_ref), (count_hbm, count_ref))
    list_copies = [
        pltpu.make_async_copy(source, target, list_sem.at[n])
        for n, (source, target) in enumerate(lists)
    ]
    for copy in list_copies:
        copy.start()

    pl.semaphore_wait(barrier, len(neighbours) + len(blk_neighbours))

    def tell(level):
        for neighbour in neighbours:
            pl.semaphore_signal(
                level_sem.at[level], inc=1, device_id={"seq": neighbour}, device_id_type=MESH
            )

    def tell_blk(level):
        for neighbour in blk_neighbours:
            pl.semaphore_signal(
                blk_sem.at[level], inc=1, device_id={"blk": neighbour}, device_id_type=MESH
            )

    tell(0)
    tell_blk(0)

    def send_keys_values(distance):
        @pl.loop(0, 2)
        def _(slot):
            for far, side in partners:
                if hops(far, side) == distance:
                    other = place(far, side)
                    pltpu.make_async_remote_copy(
                        src_ref=own_block(slot + 1, other),
                        dst_ref=kv_all.at[slot, me],
                        send_sem=kv_send.at[slot],
                        recv_sem=kv_recv.at[slot],
                        device_id={"seq": other},
                        device_id_type=MESH,
                    ).start()

    send_keys_values(1)

    pl.semaphore_wait(level_sem.at[0], len(neighbours))
    tell(1)
    send_keys_values(2)
    pl.semaphore_wait(blk_sem.at[0], len(blk_neighbours))
    tell_blk(1)

    kept_mine = pl.ds(region * kept_own, kept_own)

    pltpu.make_async_copy(kept_ref, kept_all.at[kept_mine], kept_recv).start()
    pltpu.make_async_copy(own_block(0, me), q_all.at[me], q_recv.at[me]).start()
    for slot in range(2):
        pltpu.make_async_copy(
            own_block(slot + 1, me), kv_all.at[slot, me], kv_recv.at[slot]
        ).start()

    for level in range(1, reach - 1):
        pl.semaphore_wait(level_sem.at[level], len(neighbours))
        if level < reach - 2:
            tell(level + 1)
        send_keys_values(level + 2)

    pl.semaphore_wait(blk_sem.at[1], len(blk_neighbours))
    for along, core in blk_partners:
        pltpu.make_async_remote_copy(
            src_ref=kept_ref,
            dst_ref=kept_all.at[kept_mine],
            send_sem=kept_send,
            recv_sem=kept_recv,
            device_id={"blk": blk_place(along, core)},
            device_id_type=MESH,
        ).start()

    @pl.loop(0, seq_count - 1)
    def _(step):
        other = partner(step, False)
        pltpu.make_async_remote_copy(
            src_ref=own_block(0, other),
            dst_ref=q_all.at[me],
            send_sem=q_send,
            recv_sem=q_recv.at[me],
            device_id={"seq": other},
            device_id_type=MESH,
        ).start()

    for copy in list_copies:
        copy.wait()
    pltpu.make_async_copy(kv_all.at[0], kv_all.at[0], kv_recv.at[0]).wait()
    pltpu.make_async_copy(kept_all, kept_all, kept_recv).wait()
    pltpu.make_async_copy(kv_all.at[1], kv_all.at[1], kv_recv.at[1]).wait()

    columns_mine = pl.ds(pl.multiple_of(me * width, width), width)

    def send_out(tile):
        pltpu.make_async_remote_copy(
            src_ref=mixed.at[tile],
            dst_ref=out_ref.at[:, columns_mine],
            send_sem=o_send,
            recv_sem=o_recv,
            device_id={"seq": tile},
            device_id_type=MESH,
        ).start()

    contract_last = (((1,), (1,)), ((), ()))

    @pl.loop(0, seq_count)
    def _(step):
        tile = partner(step, True)
        pltpu.make_async_copy(q_all.at[tile], q_all.at[tile], q_recv.at[tile]).wait()
        row = tile * blk_count + region
        queries = q_all[tile]
        live = count_ref[row]
        top = None
        for pair in range((near_count + window) // 2):
            first = 2 * pair
            if first < near_count:
                ids = [cur_ref[first + n, row] // blk_count for n in range(2)]
                keys = [kv_all[0, i] for i in ids]
            else:
                slots = [first - near_count + n for n in range(2)]
                keys = [kept_all[kept_list_ref[w, row], 0] for w in slots]
            product = lax.dot_general(
                queries,
                jnp.concatenate(keys, axis=0),
                contract_last,
                preferred_element_type=jnp.float32,
            )
            for n in range(2):
                part = product[:, n * width : (n + 1) * width]
                if first >= near_count + 1 or (first >= near_count and n > 0):
                    part = part + jnp.where(first - near_count + n < live, 0.0, MASKED_SCORE)
                scores[:, pl.ds((first + n) * width, width)] = part
                top = part if top is None else jnp.maximum(top, part)
        row_max = jnp.max(top, axis=1, keepdims=True)
        total = None
        mixture = None
        for pair in range((near_count + window) // 2):
            first = 2 * pair
            weight = jnp.exp2((scores[:, pl.ds(first * width, 2 * width)] - row_max) * factor)
            half = weight[:, :width] + weight[:, width:]
            total = half if total is None else total + half
            rounded = weight.astype(jnp.bfloat16)
            if first < near_count:
                ids = [cur_ref[first + n, row] // blk_count for n in range(2)]
                values = [kv_all[1, i] for i in ids]
            else:
                slots = [first - near_count + n for n in range(2)]
                values = [kept_all[kept_list_ref[w, row], 1] for w in slots]
            term = jnp.dot(
                rounded, jnp.concatenate(values, axis=0), preferred_element_type=jnp.float32
            )
            mixture = term if mixture is None else mixture + term
        row_total = jnp.sum(total, axis=1, keepdims=True)
        mixed[tile] = (mixture / row_total).astype(jnp.bfloat16)

        @pl.when(step > 0)
        def _():
            send_out(partner(step - 1, True))

    out_ref[:, columns_mine] = mixed[me]

    others = pl.ds(0, seq_count - 1)
    for send in (kv_send.at[0], kv_send.at[1], q_send, o_send):
        pltpu.make_async_copy(q_all.at[others], q_all.at[others], send).wait()
    kept_others = pl.ds(0, kept_own * (blk_count - 1))
    pltpu.make_async_copy(kept_all.at[kept_others], kept_all.at[kept_others], kept_send).wait()
    pltpu.make_async_copy(q_all.at[others], q_all.at[others], o_recv).wait()


def per_device(qkv, kept_kv, cur_list, kept_list, kept_count):
    seq_count = lax.axis_size("seq")
    blk_count = lax.axis_size("blk")
    tile_len = qkv.shape[0]
    width = HEAD_DIM
    near_count = cur_list.shape[1]
    window = kept_list.shape[1]
    block = (tile_len, width)
    hbm = pl.BlockSpec(memory_space=pltpu.HBM)
    dma = pltpu.SemaphoreType.DMA
    return pl.pallas_call(
        functools.partial(kernel, seq_count, blk_count, 4, 2),
        out_shape=jax.ShapeDtypeStruct((tile_len, seq_count * width), jnp.bfloat16),
        in_specs=[hbm] * 5,
        out_specs=pl.BlockSpec(memory_space=pltpu.VMEM),
        scratch_shapes=[
            pltpu.SMEM(cur_list.shape[::-1], jnp.int32),
            pltpu.SMEM(kept_list.shape[::-1], jnp.int32),
            pltpu.SMEM(kept_count.shape, jnp.int32),
            pltpu.VMEM((seq_count,) + block, jnp.bfloat16),
            pltpu.VMEM((2, seq_count) + block, jnp.bfloat16),
            pltpu.VMEM((kept_kv.shape[0] * blk_count, 2) + block, jnp.bfloat16),
            pltpu.VMEM((tile_len, (near_count + window) * width), jnp.float32),
            pltpu.VMEM((seq_count,) + block, jnp.bfloat16),
            dma((3,)),
            dma,
            dma,
            dma((2,)),
            dma((2,)),
            dma,
            dma((seq_count,)),
            dma,
            dma,
            pltpu.SemaphoreType.REGULAR((5,)),
            pltpu.SemaphoreType.REGULAR((2,)),
        ],
        compiler_params=pltpu.CompilerParams(
            collective_id=0, has_side_effects=True, vmem_limit_bytes=50 << 20
        ),
    )(*(pltpu.with_memory_space_constraint(a, pltpu.HBM) for a in (cur_list.T, kept_list.T, kept_count, qkv, kept_kv)))


def solution(mesh):
    placed = (P(("seq", "blk"), None), P("blk", None, None, "seq"), P(), P(), P())
    return jax.shard_map(
        per_device, mesh=mesh, in_specs=placed, out_specs=P(("seq", "blk"), None), check_vma=False
    )
```

```python
import functools
import math

import jax
import jax.numpy as jnp
from jax import lax
from jax.experimental import pallas as pl
from jax.experimental.pallas import tpu as pltpu
from jax.sharding import PartitionSpec as P

HEAD_DIM = 128
MASKED_SCORE = -1e30
MESH = pl.DeviceIdType.MESH
LOG2_E = 1.4426950408889634


def kernel(
    seq_count,
    blk_count,
    rows,
    cores,
    cur_hbm,
    kept_list_hbm,
    count_hbm,
    qkv_ref,
    kept_ref,
    out_ref,
    cur_ref,
    kept_list_ref,
    count_ref,
    q_all,
    kv_all,
    kept_all,
    scores,
    mixed,
    list_sem,
    kept_send,
    kept_recv,
    kv_send,
    kv_recv,
    q_send,
    q_recv,
    o_send,
    o_recv,
    level_sem,
    blk_sem,
):
    me = lax.axis_index("seq")
    rings = seq_count // rows
    my_z = me // rows
    my_x = lax.rem(me, rows)

    z_at = [lax.rem(my_z + far, rings) for far in range(rings)]
    x_at = [lax.rem(my_x + side, rows) for side in range(rows)]

    def place(far, side):
        return z_at[far] * rows + x_at[side]

    def hops(far, side):
        return min(far, rings - far) + min(side, rows - side)

    turns = [rings // 2]
    for far in range(rings // 2 - 1, 0, -1):
        turns += [far, rings - far]
    turns += [0]
    sides = [rows // 2]
    for side in range(rows // 2 - 1, 0, -1):
        sides += [side, rows - side]
    sides += [0]
    partners = [(far, side) for side in sides for far in turns]
    partners.remove((0, 0))
    reach = rings // 2 + rows // 2
    neighbours = [place(far, side) for far, side in partners if hops(far, side) == 1]

    def partner(step, back):
        turn = lax.rem(step, rings)
        far = (turn + 1) // 2 * (1 - 2 * lax.rem(turn, 2)) + rings // 2
        group = step // rings
        side = (group + 1) // 2 * (1 - 2 * lax.rem(group, 2)) + rows // 2
        if back:
            far, side = rings - far, rows - side
        return lax.rem(my_z + far, rings) * rows + lax.rem(my_x + side, rows)

    region = lax.axis_index("blk")
    my_y = region // cores
    my_core = lax.rem(region, cores)
    columns = blk_count // cores

    def blk_place(along, core):
        return lax.rem(my_y + along, columns) * cores + lax.rem(my_core + core, cores)

    blk_partners = [(along, core) for core in range(cores) for along in range(columns)]
    blk_partners.remove((0, 0))
    blk_neighbours = [blk_place(*at) for at in ((1, 0), (columns - 1, 0), (0, 1))]
    near_count = cur_ref.shape[0]
    window = kept_list_ref.shape[0]
    kept_own = kept_ref.shape[0]
    width = HEAD_DIM
    factor = LOG2_E / math.sqrt(width)

    barrier = pltpu.get_barrier_semaphore()

    for neighbour in neighbours:
        pl.semaphore_signal(barrier, inc=1, device_id={"seq": neighbour}, device_id_type=MESH)

    for neighbour in blk_neighbours:
        pl.semaphore_signal(barrier, inc=1, device_id={"blk": neighbour}, device_id_type=MESH)

    def own_block(group, head):
        column = pl.multiple_of((group * seq_count + head) * width, width)
        return qkv_ref.at[:, pl.ds(column, width)]

    lists = ((cur_hbm, cur_ref), (kept_list_hbm, kept_list_ref), (count_hbm, count_ref))
    list_copies = [
        pltpu.make_async_copy(source, target, list_sem.at[n])
        for n, (source, target) in enumerate(lists)
    ]
    for copy in list_copies:
        copy.start()

    pl.semaphore_wait(barrier, len(neighbours) + len(blk_neighbours))

    def tell(level):
        for neighbour in neighbours:
            pl.semaphore_signal(
                level_sem.at[level], inc=1, device_id={"seq": neighbour}, device_id_type=MESH
            )

    def tell_blk(level):
        for neighbour in blk_neighbours:
            pl.semaphore_signal(
                blk_sem.at[level], inc=1, device_id={"blk": neighbour}, device_id_type=MESH
            )

    tell(0)
    tell_blk(0)

    def send_keys_values(distance):
        @pl.loop(0, 2)
        def _(slot):
            for far, side in partners:
                if hops(far, side) == distance:
                    other = place(far, side)
                    pltpu.make_async_remote_copy(
                        src_ref=own_block(slot + 1, other),
                        dst_ref=kv_all.at[slot, me],
                        send_sem=kv_send.at[slot],
                        recv_sem=kv_recv.at[slot],
                        device_id={"seq": other},
                        device_id_type=MESH,
                    ).start()

    send_keys_values(1)

    pl.semaphore_wait(level_sem.at[0], len(neighbours))
    tell(1)
    send_keys_values(2)
    pl.semaphore_wait(blk_sem.at[0], len(blk_neighbours))
    tell_blk(1)

    kept_mine = pl.ds(region * kept_own, kept_own)

    pltpu.make_async_copy(kept_ref, kept_all.at[kept_mine], kept_recv).start()
    pltpu.make_async_copy(own_block(0, me), q_all.at[me], q_recv.at[me]).start()
    for slot in range(2):
        pltpu.make_async_copy(
            own_block(slot + 1, me), kv_all.at[slot, me], kv_recv.at[slot]
        ).start()

    for level in range(1, reach - 1):
        pl.semaphore_wait(level_sem.at[level], len(neighbours))
        if level < reach - 2:
            tell(level + 1)
        send_keys_values(level + 2)

    pl.semaphore_wait(blk_sem.at[1], len(blk_neighbours))
    for along, core in blk_partners:
        pltpu.make_async_remote_copy(
            src_ref=kept_ref,
            dst_ref=kept_all.at[kept_mine],
            send_sem=kept_send,
            recv_sem=kept_recv,
            device_id={"blk": blk_place(along, core)},
            device_id_type=MESH,
        ).start()

    @pl.loop(0, seq_count - 1)
    def _(step):
        other = partner(step, False)
        pltpu.make_async_remote_copy(
            src_ref=own_block(0, other),
            dst_ref=q_all.at[me],
            send_sem=q_send,
            recv_sem=q_recv.at[me],
            device_id={"seq": other},
            device_id_type=MESH,
        ).start()

    for copy in list_copies:
        copy.wait()
    pltpu.make_async_copy(kv_all.at[0], kv_all.at[0], kv_recv.at[0]).wait()
    pltpu.make_async_copy(kept_all, kept_all, kept_recv).wait()
    pltpu.make_async_copy(kv_all.at[1], kv_all.at[1], kv_recv.at[1]).wait()

    columns_mine = pl.ds(pl.multiple_of(me * width, width), width)

    def send_out(tile):
        pltpu.make_async_remote_copy(
            src_ref=mixed.at[tile],
            dst_ref=out_ref.at[:, columns_mine],
            send_sem=o_send,
            recv_sem=o_recv,
            device_id={"seq": tile},
            device_id_type=MESH,
        ).start()

    contract_last = (((1,), (1,)), ((), ()))

    @pl.loop(0, seq_count)
    def _(step):
        tile = partner(step, True)
        pltpu.make_async_copy(q_all.at[tile], q_all.at[tile], q_recv.at[tile]).wait()
        row = tile * blk_count + region
        queries = q_all[tile]
        live = count_ref[row]
        top = None
        for pair in range((near_count + window) // 2):
            first = 2 * pair
            if first < near_count:
                ids = [cur_ref[first + n, row] // blk_count for n in range(2)]
                keys = [kv_all[0, i] for i in ids]
            else:
                slots = [first - near_count + n for n in range(2)]
                keys = [kept_all[kept_list_ref[w, row], 0] for w in slots]
            product = lax.dot_general(
                queries,
                jnp.concatenate(keys, axis=0),
                contract_last,
                preferred_element_type=jnp.float32,
            )
            for n in range(2):
                part = product[:, n * width : (n + 1) * width]
                if first >= near_count + 1 or (first >= near_count and n > 0):
                    part = part + jnp.where(first - near_count + n < live, 0.0, MASKED_SCORE)
                scores[:, pl.ds((first + n) * width, width)] = part
                top = part if top is None else jnp.maximum(top, part)
        row_max = jnp.max(top, axis=1, keepdims=True)
        total = None
        mixture = None
        for pair in range((near_count + window) // 2):
            first = 2 * pair
            weight = jnp.exp2((scores[:, pl.ds(first * width, 2 * width)] - row_max) * factor)
            half = weight[:, :width] + weight[:, width:]
            total = half if total is None else total + half
            rounded = weight.astype(jnp.bfloat16)
            if first < near_count:
                ids = [cur_ref[first + n, row] // blk_count for n in range(2)]
                values = [kv_all[1, i] for i in ids]
            else:
                slots = [first - near_count + n for n in range(2)]
                values = [kept_all[kept_list_ref[w, row], 1] for w in slots]
            term = jnp.dot(
                rounded, jnp.concatenate(values, axis=0), preferred_element_type=jnp.float32
            )
            mixture = term if mixture is None else mixture + term
        row_total = jnp.sum(total, axis=1, keepdims=True)
        mixed[tile] = (mixture / row_total).astype(jnp.bfloat16)

        @pl.when(step > 0)
        def _():
            send_out(partner(step - 1, True))

    out_ref[:, columns_mine] = mixed[me]

    others = pl.ds(0, seq_count - 1)
    for send in (kv_send.at[0], kv_send.at[1], q_send, o_send):
        pltpu.make_async_copy(q_all.at[others], q_all.at[others], send).wait()
    kept_others = pl.ds(0, kept_own * (blk_count - 1))
    pltpu.make_async_copy(kept_all.at[kept_others], kept_all.at[kept_others], kept_send).wait()
    pltpu.make_async_copy(q_all.at[others], q_all.at[others], o_recv).wait()


def per_device(qkv, kept_kv, cur_list, kept_list, kept_count):
    seq_count = lax.axis_size("seq")
    blk_count = lax.axis_size("blk")
    tile_len = qkv.shape[0]
    width = HEAD_DIM
    near_count = cur_list.shape[1]
    window = kept_list.shape[1]
    block = (tile_len, width)
    hbm = pl.BlockSpec(memory_space=pltpu.HBM)
    dma = pltpu.SemaphoreType.DMA
    return pl.pallas_call(
        functools.partial(kernel, seq_count, blk_count, 4, 2),
        out_shape=jax.ShapeDtypeStruct((tile_len, seq_count * width), jnp.bfloat16),
        in_specs=[hbm] * 5,
        out_specs=pl.BlockSpec(memory_space=pltpu.VMEM),
        scratch_shapes=[
            pltpu.SMEM(cur_list.shape[::-1], jnp.int32),
            pltpu.SMEM(kept_list.shape[::-1], jnp.int32),
            pltpu.SMEM(kept_count.shape, jnp.int32),
            pltpu.VMEM((seq_count,) + block, jnp.bfloat16),
            pltpu.VMEM((2, seq_count) + block, jnp.bfloat16),
            pltpu.VMEM((kept_kv.shape[0] * blk_count, 2) + block, jnp.bfloat16),
            pltpu.VMEM((tile_len, (near_count + window) * width), jnp.float32),
            pltpu.VMEM((seq_count,) + block, jnp.bfloat16),
            dma((3,)),
            dma,
            dma,
            dma((2,)),
            dma((2,)),
            dma,
            dma((seq_count,)),
            dma,
            dma,
            pltpu.SemaphoreType.REGULAR((5,)),
            pltpu.SemaphoreType.REGULAR((2,)),
        ],
        compiler_params=pltpu.CompilerParams(
            collective_id=0, has_side_effects=True, vmem_limit_bytes=50 << 20
        ),
    )(*(pltpu.with_memory_space_constraint(a, pltpu.HBM) for a in (cur_list.T, kept_list.T, kept_count, qkv, kept_kv)))


def solution(mesh):
    placed = (P(("seq", "blk"), None), P("blk", None, None, "seq"), P(), P(), P())
    return jax.shard_map(
        per_device, mesh=mesh, in_specs=placed, out_specs=P(("seq", "blk"), None), check_vma=False
    )
```
